256 devices in a mesh: section: 8 (over z_hi, core), tp: 32 (over z_lo, x, y).
Axes of the slice: x: 4, y: 4, z: 8 (z_hi: 4, z_lo: 2; z = z_hi * 2 + z_lo), core: 2. Of those that a mesh axis runs over, the one named last changes fastest.
Arguments:
- start_tokens: bfloat16 [2, 32, 8192], P(None, None, 'tp'), may hold values from -6 to 6
- target_weight: bfloat16 [8, 8192, 8192], P('section', None, 'tp'), may hold values from -0.0625 to 0.0625
- online_weight: bfloat16 [8, 8192, 8192], P('section', 'tp'), may hold values from -0.0625 to 0.0625
- head_weight: bfloat16 [8192, 256], P('tp'), may hold values from -0.0625 to 0.0625
- reward: float32 [2, 32], P(None, 'section'), may hold values from -6 to 6
- action_bin: int32 [2, 32], P(None, 'section'), may hold values from 0 to 255
Outputs:
- target_value: float32 [2, 32], P(None, 'section')
- q_taken: float32 [2, 32], P(None, 'section')
The draws below stay inside these ranges and needn't reach their ends.
All inputs are finite; a program needn't handle non-finite values.
Results may differ from the reference program's by a relative error of at most 0.018.
Values may be sent and summed in bfloat16 or wider, within the bound.
A program may use at most 64 MiB of HBM per device.

```python
import jax
import jax.numpy as jnp
from jax import lax

D = 8192
BINS = 256
ROWS = 32
MICRO = 2
LAYERS = 8


def touch_ends(drawn, rng, smallest, high):
    extent = drawn.shape
    spot = [jax.random.randint(jax.random.fold_in(rng, axis), (), 0, extent[axis]) for axis in range(len(extent))]
    drawn = drawn.at[tuple(spot)].set(smallest)
    longest = extent.index(max(extent))
    spot[longest] = (spot[longest] + 1) % extent[longest]
    return drawn.at[tuple(spot)].set(high)


def steps_of(key, dims, shards, low, high):
    level = 1.0
    for dim, parts in shards:
        draws = jax.random.uniform(jax.random.fold_in(jax.random.fold_in(key, 6), dim), (parts,), jnp.float32, low / len(shards), high / len(shards))
        level = level * jnp.repeat(jnp.exp(draws), dims[dim] // parts).reshape((-1,) + (1,) * (len(dims) - 1 - dim))
    return level


def normal_values(stream_key, extent, width, most, shards=(), held_as=jnp.bfloat16):
    values = jax.random.normal(stream_key, extent, jnp.float32) * width
    if len(shards) > 0:
        values = steps_of(stream_key, extent, shards, -0.22, 0.18) * values
    return jnp.clip(values, min=-most, max=most).astype(held_as)


def setup_inputs(seed: int = 0) -> dict:
    keys = jax.random.split(jax.random.key(seed), 7)
    return {
        "start_tokens": normal_values(keys[0], (MICRO, ROWS, D), 1.0, 6.0, ((2, 32),)),
        "target_weight": normal_values(keys[1], (LAYERS, D, D), D ** -0.5, 0.0625, ((0, 8), (2, 32))),
        "online_weight": normal_values(keys[2], (LAYERS, D, D), D ** -0.5, 0.0625, ((0, 8), (1, 32))),
        "head_weight": normal_values(keys[3], (D, BINS), D ** -0.5, 0.0625, ((0, 32),)),
        "reward": normal_values(keys[4], (MICRO, ROWS), 1.0, 6.0, ((1, 8),), jnp.float32),
        "action_bin": touch_ends(jax.random.randint(keys[5], (MICRO, ROWS), 0, BINS), jax.random.fold_in(keys[5], 1), 0, BINS - 1).astype(jnp.int32),
    }


def reference(start_tokens, target_weight, online_weight, head_weight, reward, action_bin):
    hidden = start_tokens.reshape(MICRO * ROWS, D)
    for layer in range(LAYERS):
        blended = (0.25 * online_weight[layer].astype(jnp.float32) + 0.75 * target_weight[layer].astype(jnp.float32)).astype(jnp.bfloat16)
        wide = hidden.astype(jnp.float32)
        normed = (wide * lax.rsqrt(lax.optimization_barrier(jnp.mean(wide * wide, axis=1, keepdims=True)) + 1e-06)).astype(jnp.bfloat16)
        hidden = (wide + jnp.dot(normed, blended, preferred_element_type=jnp.float32)).astype(jnp.bfloat16)
    values = jnp.dot(hidden, head_weight, preferred_element_type=jnp.float32)
    best = lax.optimization_barrier(jnp.max(values, axis=1)).reshape(MICRO, ROWS)
    chosen = (jnp.arange(BINS, dtype=jnp.int32)[None, :] == action_bin.reshape(MICRO * ROWS, 1)).astype(jnp.float32)
    taken = lax.optimization_barrier(jnp.sum(values * chosen, axis=1)).reshape(MICRO, ROWS)
    return (reward + 0.98 * best, taken)
```

```python
import functools

import jax
import jax.numpy as jnp
from jax import lax
from jax.experimental import pallas as pl
from jax.experimental.pallas import tpu as pltpu
from jax.sharding import PartitionSpec as P

MESH = pl.DeviceIdType.MESH
SECTIONS = 8
PEERS = 32
ROWS = 64
WIDTH = 256
DEPTH = PEERS * WIDTH
CHUNKS = 4
AHEAD = 2
PART = ROWS // CHUNKS
OWNED = 8


def place(tp):
    return tp // 16, lax.rem(tp // 4, 4), lax.rem(tp, 4)


def index(z, x, y):
    return z * 16 + x * 4 + y


def far(v):
    return v + v // 2 - 2 * (v // 3)


def peer(tp, step):
    z, x, y = place(tp)
    return index(
        lax.rem(z + step // 16, 2),
        lax.rem(x + far(lax.rem(step // 4, 4)), 4),
        lax.rem(y + far(lax.rem(step, 4)), 4),
    )


def kernel(
    start_ref, target_ref, online_ref, head_ref, reward_ref, action_ref, value_ref, taken_ref,
    target, online, hidden, shares, sends, result, scores, gathered, summed, finals,
    load_sem, own_sem, all_sem, share_sem, all_out, next_out, share_out, score_sem, score_out, final_sem, final_out,
):
    section = lax.axis_index("section")
    me = lax.axis_index("tp")
    z, x, y = place(me)
    odd = lax.rem(section, 2)
    even = odd == 0
    last = section == SECTIONS - 1
    my_micro, bit = y // 2, lax.rem(y, 2)
    my_block = (1 - bit) * (1 - z) + bit * (2 + z)

    def owner(micro, block):
        return index(lax.rem((block + 1) // 2 + 1, 2), x, 2 * micro + block // 2)

    def remote(src, dst, out, sem, at_section, tp):
        return pltpu.make_async_remote_copy(
            src_ref=src, dst_ref=dst, send_sem=out, recv_sem=sem,
            device_id={"section": at_section, "tp": tp}, device_id_type=MESH,
        )

    def settle(ref, sem):
        pltpu.make_async_copy(ref, ref, sem).wait()

    load_online = pltpu.make_async_copy(online_ref, online, load_sem.at[0])
    load_target = pltpu.make_async_copy(target_ref, target, load_sem.at[1])
    load_online.start()
    load_target.start()

    @pl.when(section == 0)
    def _():
        for c in range(CHUNKS):
            pltpu.make_async_copy(
                start_ref.at[pl.ds(c * PART, PART)], hidden.at[c, me], own_sem.at[c]
            ).start()

    barrier = pltpu.get_barrier_semaphore()

    def greet(at_section, tp):
        pl.semaphore_signal(
            barrier, inc=1, device_id={"section": at_section, "tp": tp}, device_id_type=MESH
        )

    @pl.loop(1, PEERS)
    def _(i):
        greet(section, peer(me, PEERS - i))

    @pl.when(odd == 1)
    def _():
        @pl.loop(0, PEERS)
        def _(i):
            greet(section - 1, peer(me, PEERS - 1 - i))

    @pl.when(jnp.logical_and(even, section > 0))
    def _():
        greet(section - 1, me)

    for micro in range(2):
        mine = owner(micro, section // 2)

        @pl.when(jnp.logical_not(jnp.logical_and(last, mine == me)))
        def _():
            greet(SECTIONS - 1, mine)

    @pl.when(even)
    def _():
        pl.semaphore_wait(barrier, 2 * PEERS - 1)

    @pl.when(jnp.logical_and(odd == 1, section < SECTIONS - 1))
    def _():
        pl.semaphore_wait(barrier, PEERS)

    @pl.when(jnp.logical_and(last, my_block != 3))
    def _():
        pl.semaphore_wait(barrier, PEERS - 1 + 16)

    @pl.when(jnp.logical_and(last, my_block == 3))
    def _():
        pl.semaphore_wait(barrier, PEERS - 1 + 15)

    load_online.wait()
    load_target.wait()

    def send(c):
        settle(hidden.at[c, 0], own_sem.at[c])

        @pl.when(even)
        def _():
            @pl.loop(1, PEERS)
            def _(i):
                remote(
                    hidden.at[c, me], hidden.at[c, me], all_out.at[c], all_sem.at[c], section, peer(me, PEERS - i)
                ).start()

        own = hidden[c, me]
        for group in range(4):
            steps = [PEERS - 1 - 8 * group - u for u in range(8)]
            for step in steps:
                tp = peer(me, step)
                part = jnp.dot(
                    own,
                    online[:, pl.ds(pl.multiple_of(tp * WIDTH, WIDTH), WIDTH)],
                    preferred_element_type=jnp.float32,
                ).astype(jnp.bfloat16)
                if step == 0:
                    shares[c, me] = part
                else:
                    sends[c, tp] = part
            for step in steps:
                if step > 0:
                    tp = peer(me, step)
                    remote(
                        sends.at[c, tp], shares.at[c, me], share_out.at[c], share_sem.at[c], section, tp
                    ).start()

    def reduce(c):
        settle(hidden.at[c, pl.ds(0, PEERS - 1)], all_sem.at[c])
        product = jnp.zeros((PART, WIDTH), jnp.float32)
        square = jnp.zeros((PART, WIDTH), jnp.float32)
        for tp in range(PEERS):
            block = hidden[c, tp]
            product += jnp.dot(
                block, target[pl.ds(tp * WIDTH, WIDTH), :], preferred_element_type=jnp.float32
            )
            wide = block.astype(jnp.float32)
            square += wide * wide
        scale = lax.rsqrt(jnp.sum(square, axis=1, keepdims=True) * (1.0 / DEPTH) + 1e-06)
        settle(shares.at[c, pl.ds(0, PEERS - 1)], share_sem.at[c])
        total = jnp.zeros((PART, WIDTH), jnp.float32)
        for tp in range(PEERS):
            total += shares[c, tp].astype(jnp.float32)
        out = (
            hidden[c, me].astype(jnp.float32) + scale * (0.75 * product + 0.25 * total)
        ).astype(jnp.bfloat16)
        result[c] = out

        @pl.when(even)
        def _():
            @pl.loop(0, PEERS - 1)
            def _(i):
                remote(
                    result.at[c], hidden.at[c, me], next_out.at[c], all_sem.at[c], section + 1, peer(me, PEERS - 1 - i)
                ).start()

        @pl.when(section < SECTIONS - 1)
        def _():
            remote(
                result.at[c], hidden.at[c, me], next_out.at[c], own_sem.at[c], section + 1, me
            ).start()

        @pl.when(last)
        def _():
            partial = jnp.dot(out, head_ref[...], preferred_element_type=jnp.float32)
            for half in range(PART // OWNED):
                group = c * (PART // OWNED) + half
                rows = partial[half * OWNED : (half + 1) * OWNED]
                scores[group] = rows
                first = owner(group // 4, lax.rem(group, 4))
                for column in range(4):
                    tp = first + (column - x) * 4

                    @pl.when(tp == me)
                    def _():
                        gathered[me] = rows

                    @pl.when(tp != me)
                    def _():
                        remote(
                            scores.at[group], gathered.at[me], score_out, score_sem, section, tp
                        ).start()

    @pl.loop(0, CHUNKS + AHEAD)
    def _(step):
        @pl.when(step < CHUNKS)
        def _():
            send(step)

        @pl.when(step >= AHEAD)
        def _():
            reduce(step - AHEAD)

    @pl.when(last)
    def _():
        settle(gathered.at[pl.ds(0, PEERS - 1)], score_sem)
        total = jnp.zeros((OWNED, WIDTH), jnp.float32)
        for tp in range(PEERS):
            total += gathered[tp]
        summed[...] = total
        for i in range(16):
            at_section = 2 * my_block + i // 8
            tp = index((i // 4) % 2, x, i % 4)
            local = jnp.logical_and(at_section == section, tp == me)

            @pl.when(local)
            def _():
                pltpu.make_async_copy(summed, finals.at[my_micro], final_sem.at[my_micro]).start()

            @pl.when(jnp.logical_not(local))
            def _():
                remote(
                    summed, finals.at[my_micro], final_out, final_sem.at[my_micro], at_section, tp
                ).start()

    lane = lax.broadcasted_iota(jnp.int32, (OWNED, WIDTH), 1)
    row = lax.broadcasted_iota(jnp.int32, (OWNED, WIDTH), 0) - 4 * odd
    for micro in range(2):
        settle(finals.at[micro], final_sem.at[micro])
        q = finals[micro]
        action = jnp.zeros((OWNED, WIDTH), jnp.int32)
        for token in range(4):
            action = jnp.where(row == token, action_ref[micro, token], action)
        best = jnp.max(q, axis=1, keepdims=True)
        taken = jnp.sum(jnp.where(lane == action, q, 0.0), axis=1, keepdims=True)
        best = jnp.sum(jnp.where(lane == row, best, 0.0), axis=0, keepdims=True)
        taken = jnp.sum(jnp.where(lane == row, taken, 0.0), axis=0, keepdims=True)
        value_ref[pl.ds(micro, 1), :] = reward_ref[pl.ds(micro, 1), :] + 0.98 * best[:, :4]
        taken_ref[pl.ds(micro, 1), :] = taken[:, :4]

    most = PEERS - 1

    @pl.loop(0, CHUNKS)
    def _(c):
        settle(sends.at[c, pl.ds(0, most)], share_out.at[c])

        @pl.when(even)
        def _():
            settle(hidden.at[c, pl.ds(0, most)], all_out.at[c])
            settle(hidden.at[c], next_out.at[c])

        @pl.when(jnp.logical_and(odd == 1, section < SECTIONS - 1))
        def _():
            settle(hidden.at[c, 0], next_out.at[c])

    @pl.when(last)
    def _():
        settle(gathered.at[pl.ds(0, most)], score_out)

        @pl.when(my_block != 3)
        def _():
            settle(gathered.at[pl.ds(0, 16)], final_out)

        @pl.when(my_block == 3)
        def _():
            settle(gathered.at[pl.ds(0, 15)], final_out)


def per_device(start_tokens, target_weight, online_weight, head_weight, reward, action_bin):
    bf16, f32 = jnp.bfloat16, jnp.float32
    dma = pltpu.SemaphoreType.DMA
    shape = jax.ShapeDtypeStruct(reward.shape, f32)
    anywhere = pl.BlockSpec(memory_space=pl.ANY)
    vmem = pl.BlockSpec(memory_space=pltpu.VMEM)
    blocks = pltpu.VMEM((CHUNKS, PEERS, PART, WIDTH), bf16)
    return pl.pallas_call(
        kernel,
        out_shape=(shape, shape),
        in_specs=[anywhere, anywhere, anywhere, vmem, vmem, pl.BlockSpec(memory_space=pltpu.SMEM)],
        out_specs=(vmem, vmem),
        scratch_shapes=[
            pltpu.VMEM((DEPTH, WIDTH), bf16),
            pltpu.VMEM((WIDTH, DEPTH), bf16),
            blocks,
            blocks,
            blocks,
            pltpu.VMEM((CHUNKS, PART, WIDTH), bf16),
            pltpu.VMEM((ROWS // OWNED, OWNED, WIDTH), f32),
            pltpu.VMEM((PEERS, OWNED, WIDTH), f32),
            pltpu.VMEM((OWNED, WIDTH), f32),
            pltpu.VMEM((2, OWNED, WIDTH), f32),
            dma((2,)),
            dma((CHUNKS,)),
            dma((CHUNKS,)),
            dma((CHUNKS,)),
            dma((CHUNKS,)),
            dma((CHUNKS,)),
            dma((CHUNKS,)),
            dma,
            dma,
            dma((2,)),
            dma,
        ],
        name="relay",
        compiler_params=pltpu.CompilerParams(collective_id=0, has_side_effects=True),
    )(
        start_tokens.reshape(ROWS, WIDTH),
        target_weight.reshape(DEPTH, WIDTH),
        online_weight.reshape(WIDTH, DEPTH),
        head_weight,
        reward,
        action_bin,
    )


def solution(mesh):
    in_specs = (
        P(None, None, "tp"),
        P("section", None, "tp"),
        P("section", "tp", None),
        P("tp", None),
        P(None, "section"),
        P(None, "section"),
    )
    out_specs = (P(None, "section"), P(None, "section"))
    return jax.shard_map(
        per_device, mesh=mesh, in_specs=in_specs, out_specs=out_specs, check_vma=False
    )
```

```python
import functools

import jax
import jax.numpy as jnp
from jax import lax
from jax.experimental import pallas as pl
from jax.experimental.pallas import tpu as pltpu
from jax.sharding import PartitionSpec as P

MESH = pl.DeviceIdType.MESH
SECTIONS = 8
PEERS = 32
ROWS = 64
WIDTH = 256
DEPTH = PEERS * WIDTH
CHUNKS = 8
AHEAD = (2, 1, 1)
PART = ROWS // CHUNKS
OWNED = 8
SCORE = 2 * WIDTH + 128
WHOLE = ()


FAR = (0, 1, 3, 2)


def place(tp):
    return tp // 16, lax.rem(tp // 4, 4), lax.rem(tp, 4)


def index(z, x, y):
    return z * 16 + x * 4 + y


def kernel(
    start_ref, target_ref, online_ref, head_ref, reward_ref, action_ref, value_ref, taken_ref,
    target, online, moved, hidden, shares, sends, result, product_head, both, scores, gathered, summed, finals, wide_finals,
    load_sem, move_sem, head_sem, row_sem, own_sem, all_sem, share_sem, move_out, all_out, next_out, share_out, score_sem, score_out, final_sem, final_out,
):
    section = lax.axis_index("section")
    me = lax.axis_index("tp")
    z, x, y = place(me)
    along_z = [z * 16, (1 - z) * 16]
    ring_x = [lax.rem(x + i, 4) * 4 for i in range(4)]
    ring_y = [lax.rem(y + i, 4) for i in range(4)]
    along_x = [ring_x[i] for i in FAR]
    along_y = [ring_y[i] for i in FAR]

    def peer(step):
        return along_z[step // 16] + along_x[step // 4 % 4] + along_y[step % 4]

    peers = range(PEERS - 1, 0, -1)
    odd = lax.rem(section, 2)
    even = odd == 0
    last = section == SECTIONS - 1
    spread = jnp.logical_and(even, section < SECTIONS - 2)
    whole = functools.reduce(jnp.logical_or, [section == s for s in WHOLE], False)
    split = jnp.logical_not(jnp.logical_or(whole, last))
    my_micro, bit = y // 2, lax.rem(y, 2)
    my_block = (1 - bit) * (1 - z) + bit * (2 + z)

    def owner(micro, block):
        return index(lax.rem((block + 1) // 2 + 1, 2), x, 2 * micro + block // 2)

    def remote(src, dst, out, sem, at_section, tp):
        return pltpu.make_async_remote_copy(
            src_ref=src, dst_ref=dst, send_sem=out, recv_sem=sem,
            device_id={"section": at_section, "tp": tp}, device_id_type=MESH,
        )

    def settle(ref, sem):
        pltpu.make_async_copy(ref, ref, sem).wait()

    def columns(tp):
        return pl.ds(pl.multiple_of(tp * WIDTH, WIDTH), WIDTH)

    load_online = pltpu.make_async_copy(online_ref, online, load_sem.at[0])
    load_online.start()

    @pl.when(jnp.logical_not(last))
    def _():
        pltpu.make_async_copy(target_ref, target, load_sem.at[1]).start()

    @pl.when(last)
    def _():
        pltpu.make_async_copy(target_ref.at[me], target.at[me], load_sem.at[1]).start()
        pltpu.make_async_copy(head_ref, moved.at[me], load_sem.at[2]).start()

    @pl.when(whole)
    def _():
        pltpu.make_async_copy(online_ref.at[:, columns(me)], moved.at[me], load_sem.at[2]).start()

    @pl.when(section == 0)
    def _():
        for c in range(CHUNKS):
            pltpu.make_async_copy(
                start_ref.at[pl.ds(c * PART, PART)], hidden.at[c, me], own_sem.at[c]
            ).start()

    barrier = pltpu.get_barrier_semaphore()

    def greet(at_section, tp):
        pl.semaphore_signal(
            barrier, inc=1, device_id={"section": at_section, "tp": tp}, device_id_type=MESH
        )

    for step in peers:
        greet(section, peer(step))

    @pl.when(jnp.logical_and(odd == 1, jnp.logical_not(last)))
    def _():
        for step in peers:
            greet(section - 1, peer(step))

    @pl.when(section > 0)
    def _():
        greet(section - 1, me)

    for micro in range(2):
        mine = owner(micro, section // 2)

        @pl.when(jnp.logical_not(jnp.logical_and(last, mine == me)))
        def _():
            greet(SECTIONS - 1, mine)

    @pl.when(spread)
    def _():
        pl.semaphore_wait(barrier, 2 * PEERS - 1)

    @pl.when(jnp.logical_not(jnp.logical_or(spread, last)))
    def _():
        pl.semaphore_wait(barrier, PEERS)

    @pl.when(jnp.logical_and(last, my_block != 3))
    def _():
        pl.semaphore_wait(barrier, PEERS - 1 + 16)

    @pl.when(jnp.logical_and(last, my_block == 3))
    def _():
        pl.semaphore_wait(barrier, PEERS - 1 + 15)

    most = PEERS - 1

    @pl.when(jnp.logical_not(last))
    def _():
        @pl.when(whole)
        def _():
            for step in peers:
                tp = peer(step)
                remote(online_ref.at[:, columns(tp)], moved.at[me], move_out, move_sem, section, tp).start()

        load_online.wait()
        settle(target, load_sem.at[1])

        @pl.when(whole)
        def _():
            settle(moved.at[0], load_sem.at[2])
            settle(moved.at[pl.ds(0, most)], move_sem)

            @pl.loop(0, PEERS)
            def _(tp):
                target[tp] = (
                    0.25 * moved[tp].astype(jnp.float32) + 0.75 * target[tp].astype(jnp.float32)
                ).astype(jnp.bfloat16)

    @pl.when(last)
    def _():
        seen = set()

        def near(dx, dy, dz):
            return along_z[dz] + ring_x[dx % 4] + ring_y[dy % 4]

        def arrived(dx, dy, dz):
            if (dx, dy, dz) not in seen:
                seen.add((dx, dy, dz))
                tp = near(dx, dy, dz)
                settle(moved.at[tp], head_sem.at[tp])

        def give_target(dx):
            for dz in (1, 0):
                for dy in (2, 1, 3, 0):
                    if (dx, dy, dz) != (0, 0, 0):
                        tp = near(dx, dy, dz)
                        remote(target_ref.at[tp], target.at[me], move_out, row_sem.at[me], section, tp).start()

        def pass_on(source, step):
            arrived(*source)
            tp = near(*source)
            remote(moved.at[tp], moved.at[tp], move_out, head_sem.at[tp], section, near(*step)).start()

        for dz in (1, 0):
            for dx in (1, 3, 0):
                for dy in (1, 3, 0):
                    if (dx, dy, dz) != (0, 0, 0):
                        remote(
                            head_ref, moved.at[me], move_out, head_sem.at[me], section, near(dx, dy, dz)
                        ).start()
        give_target(0)
        for dx in (1, 0, 3):
            for dz in (0, 1):
                pass_on((dx, 1, dz), (0, -1, 0))
        give_target(1)
        for dy in (0, 1, 3, 2):
            for dz in (0, 1):
                pass_on((1, dy, dz), (-1, 0, 0))
        give_target(3)
        give_target(2)
        load_online.wait()
        settle(target.at[0], load_sem.at[1])
        settle(moved.at[0], load_sem.at[2])
        product_head[...] = jnp.zeros_like(product_head)
        for dx in (0, 1, 3, 2):
            for dz in range(2):
                for dy in range(4):
                    if (dx, dy, dz) != (0, 0, 0):
                        arrived(dx, dy, dz)
                        tp = near(dx, dy, dz)
                        settle(target.at[tp], row_sem.at[tp])

            @pl.loop(0, 8)
            def _(i):
                tp = (i // 4) * 16 + ring_x[dx] + lax.rem(i, 4)
                blended = (
                    0.25 * online[:, columns(tp)].astype(jnp.float32) + 0.75 * target[tp].astype(jnp.float32)
                ).astype(jnp.bfloat16)
                product_head[...] += jnp.dot(blended, moved[tp], preferred_element_type=jnp.float32)

        both[:, :WIDTH] = moved[me]
        both[:, WIDTH:] = product_head[...].astype(jnp.bfloat16)

    def send(c):
        @pl.when(jnp.logical_or(even, split))
        def _():
            settle(hidden.at[c, 0], own_sem.at[c])

        @pl.when(even)
        def _():
            for step in peers:
                remote(
                    hidden.at[c, me], hidden.at[c, me], all_out.at[c], all_sem.at[c], section, peer(step)
                ).start()

        @pl.when(split)
        def _():
            own = hidden[c, me]
            for group in range(4):
                steps = [PEERS - 1 - 8 * group - u for u in range(8)]
                for step in steps:
                    tp = peer(step)
                    part = jnp.dot(
                        own, online[:, columns(tp)], preferred_element_type=jnp.float32
                    ).astype(jnp.bfloat16)
                    if step == 0:
                        shares[c, me] = part
                    else:
                        sends[c, tp] = part
                for step in steps:
                    if step > 0:
                        tp = peer(step)
                        remote(
                            sends.at[c, tp], shares.at[c, me], share_out.at[c], share_sem.at[c], section, tp
                        ).start()

    def reduce(c):
        @pl.when(jnp.logical_not(jnp.logical_or(even, split)))
        def _():
            settle(hidden.at[c, 0], own_sem.at[c])

        settle(hidden.at[c, pl.ds(0, most)], all_sem.at[c])
        product = jnp.zeros((PART, WIDTH), jnp.float32)
        square = jnp.zeros((PART, WIDTH), jnp.float32)
        for tp in range(PEERS):
            block = hidden[c, tp]
            product += jnp.dot(block, target[tp], preferred_element_type=jnp.float32)
            wide = block.astype(jnp.float32)
            square += wide * wide
        scale = lax.rsqrt(jnp.sum(square, axis=1, keepdims=True) * (1.0 / DEPTH) + 1e-06)
        own = hidden[c, me].astype(jnp.float32)

        @pl.when(split)
        def _():
            settle(shares.at[c, pl.ds(0, most)], share_sem.at[c])
            total = jnp.zeros((PART, WIDTH), jnp.float32)
            for tp in range(PEERS):
                total += shares[c, tp].astype(jnp.float32)
            result[c] = (own + scale * (0.75 * product + 0.25 * total)).astype(jnp.bfloat16)

        @pl.when(whole)
        def _():
            result[c] = (own + scale * product).astype(jnp.bfloat16)

        @pl.when(spread)
        def _():
            for step in peers:
                remote(
                    result.at[c], hidden.at[c, me], next_out.at[c], all_sem.at[c], section + 1, peer(step)
                ).start()

        remote(result.at[c], hidden.at[c, me], next_out.at[c], own_sem.at[c], section + 1, me).start()

    @pl.when(jnp.logical_not(last))
    def _():
        ahead = jnp.where(section == 0, AHEAD[0], jnp.where(even, AHEAD[2], AHEAD[1]))

        @pl.loop(0, CHUNKS + max(AHEAD))
        def _(step):
            @pl.when(step < CHUNKS)
            def _():
                send(step)

            @pl.when(jnp.logical_and(step >= ahead, step < CHUNKS + ahead))
            def _():
                reduce(step - ahead)

    @pl.when(last)
    def _():
        @pl.loop(0, CHUNKS)
        def _(c):
            settle(hidden.at[c, 0], own_sem.at[c])
            own = hidden[c, me]
            wide = own.astype(jnp.float32)
            scores[c, :, : 2 * WIDTH] = jnp.dot(own, both[...], preferred_element_type=jnp.float32)
            scores[c, :, 2 * WIDTH :] = jnp.broadcast_to(
                jnp.sum(wide * wide, axis=1, keepdims=True), (OWNED, 128)
            )
            first = owner(c // 4, lax.rem(c, 4))
            for column in range(4):
                tp = first + (column - x) * 4

                @pl.when(tp == me)
                def _():
                    gathered[me] = scores[c]

                @pl.when(tp != me)
                def _():
                    remote(scores.at[c], gathered.at[me], score_out, score_sem, section, tp).start()

        settle(gathered.at[pl.ds(0, most)], score_sem)
        total = jnp.zeros((OWNED, SCORE), jnp.float32)
        for tp in range(PEERS):
            total += gathered[tp]
        scale = lax.rsqrt(total[:, 2 * WIDTH : 2 * WIDTH + 1] * (1.0 / DEPTH) + 1e-06)
        summed[...] = total[:, :WIDTH] + scale * total[:, WIDTH : 2 * WIDTH]
        for i in range(16):
            at_section = 2 * my_block + i // 8
            tp = index((i // 4) % 2, x, i % 4)
            local = jnp.logical_and(at_section == section, tp == me)

            @pl.when(local)
            def _():
                pltpu.make_async_copy(summed, finals.at[my_micro], final_sem.at[my_micro]).start()

            @pl.when(jnp.logical_not(local))
            def _():
                remote(
                    summed, finals.at[my_micro], final_out, final_sem.at[my_micro], at_section, tp
                ).start()

    @pl.loop(0, CHUNKS)
    def _(c):
        @pl.when(split)
        def _():
            settle(sends.at[c, pl.ds(0, most)], share_out.at[c])

        @pl.when(even)
        def _():
            settle(hidden.at[c, pl.ds(0, most)], all_out.at[c])

        @pl.when(spread)
        def _():
            settle(hidden.at[c], next_out.at[c])

        @pl.when(jnp.logical_not(jnp.logical_or(spread, last)))
        def _():
            settle(hidden.at[c, 0], next_out.at[c])

    @pl.when(whole)
    def _():
        settle(moved.at[pl.ds(0, most)], move_out)

    @pl.when(last)
    def _():
        settle(moved.at[pl.ds(0, most)], move_out)
        settle(target.at[pl.ds(0, most)], move_out)

    lane = lax.broadcasted_iota(jnp.int32, (OWNED, WIDTH), 1)
    row = lax.broadcasted_iota(jnp.int32, (OWNED, WIDTH), 0) - 4 * odd
    for micro in range(2):
        settle(finals.at[micro], final_sem.at[micro])
        q = finals[micro]
        action = jnp.zeros((OWNED, WIDTH), jnp.int32)
        for token in range(4):
            action = jnp.where(row == token, action_ref[micro, token], action)
        best = jnp.max(q, axis=1, keepdims=True)
        taken = jnp.sum(jnp.where(lane == action, q, 0.0), axis=1, keepdims=True)
        best = jnp.sum(jnp.where(lane == row, best, 0.0), axis=0, keepdims=True)
        taken = jnp.sum(jnp.where(lane == row, taken, 0.0), axis=0, keepdims=True)
        value_ref[pl.ds(micro, 1), :] = reward_ref[pl.ds(micro, 1), :] + 0.98 * best[:, :4]
        taken_ref[pl.ds(micro, 1), :] = taken[:, :4]

    @pl.when(last)
    def _():
        settle(gathered.at[pl.ds(0, most)], score_out)

        @pl.when(my_block != 3)
        def _():
            settle(wide_finals.at[pl.ds(0, 16)], final_out)

        @pl.when(my_block == 3)
        def _():
            settle(wide_finals.at[pl.ds(0, 15)], final_out)


def per_device(start_tokens, target_weight, online_weight, head_weight, reward, action_bin):
    bf16, f32 = jnp.bfloat16, jnp.float32
    dma = pltpu.SemaphoreType.DMA
    shape = jax.ShapeDtypeStruct(reward.shape, f32)
    anywhere = pl.BlockSpec(memory_space=pl.ANY)
    vmem = pl.BlockSpec(memory_space=pltpu.VMEM)
    blocks = pltpu.VMEM((CHUNKS, PEERS, PART, WIDTH), bf16)
    weight = pltpu.VMEM((PEERS, WIDTH, WIDTH), bf16)
    return pl.pallas_call(
        kernel,
        out_shape=(shape, shape),
        in_specs=[anywhere, anywhere, anywhere, anywhere, vmem, pl.BlockSpec(memory_space=pltpu.SMEM)],
        out_specs=(vmem, vmem),
        scratch_shapes=[
            weight,
            pltpu.VMEM((WIDTH, DEPTH), bf16),
            weight,
            blocks,
            blocks,
            blocks,
            pltpu.VMEM((CHUNKS, PART, WIDTH), bf16),
            pltpu.VMEM((WIDTH, WIDTH), f32),
            pltpu.VMEM((WIDTH, 2 * WIDTH), bf16),
            pltpu.VMEM((CHUNKS, OWNED, SCORE), f32),
            pltpu.VMEM((PEERS, OWNED, SCORE), f32),
            pltpu.VMEM((OWNED, WIDTH), f32),
            pltpu.VMEM((2, OWNED, WIDTH), f32),
            pltpu.VMEM((16, OWNED, WIDTH), f32),
            dma((3,)),
            dma,
            dma((PEERS,)),
            dma((PEERS,)),
            dma((CHUNKS,)),
            dma((CHUNKS,)),
            dma((CHUNKS,)),
            dma,
            dma((CHUNKS,)),
            dma((CHUNKS,)),
            dma((CHUNKS,)),
            dma,
            dma,
            dma((2,)),
            dma,
        ],
        name="relay",
        compiler_params=pltpu.CompilerParams(collective_id=0, has_side_effects=True),
    )(
        start_tokens.reshape(ROWS, WIDTH),
        target_weight.reshape(PEERS, WIDTH, WIDTH),
        online_weight.reshape(WIDTH, DEPTH),
        head_weight,
        reward,
        action_bin,
    )


def solution(mesh):
    in_specs = (
        P(None, None, "tp"),
        P("section", None, "tp"),
        P("section", "tp", None),
        P("tp", None),
        P(None, "section"),
        P(None, "section"),
    )
    out_specs = (P(None, "section"), P(None, "section"))
    return jax.shard_map(
        per_device, mesh=mesh, in_specs=in_specs, out_specs=out_specs, check_vma=False
    )
```

```python
import jax
import jax.numpy as jnp
from jax import lax
from jax.experimental import pallas as pl
from jax.experimental.pallas import tpu as pltpu
from jax.sharding import PartitionSpec as P

MESH = pl.DeviceIdType.MESH
SECTIONS = 8
PEERS = 32
ROWS = 64
WIDTH = 256
DEPTH = PEERS * WIDTH
CHUNKS = 8
AHEAD = (2, 1, 1)
PART = ROWS // CHUNKS
OWNED = 8
SCORE = 2 * WIDTH + 128
FIRST = 4


FAR = (0, 1, 3, 2)


def place(tp):
    return tp // 16, lax.rem(tp // 4, 4), lax.rem(tp, 4)


def index(z, x, y):
    return z * 16 + x * 4 + y


def kernel(
    start_ref, target_ref, online_ref, head_ref, action_ref, out_ref,
    target, online, moved, hidden, shares, sends, result, product_head, both, scores, gathered, summed, finals, wide_finals,
    load_sem, head_sem, row_sem, own_sem, all_sem, share_sem, move_out, all_out, next_out, share_out, score_sem, score_out, final_sem, final_out,
):
    section = lax.axis_index("section")
    me = lax.axis_index("tp")
    z, x, y = place(me)
    along_z = [z * 16, (1 - z) * 16]
    ring_x = [lax.rem(x + i, 4) * 4 for i in range(4)]
    ring_y = [lax.rem(y + i, 4) for i in range(4)]
    along_x = [ring_x[i] for i in FAR]
    along_y = [ring_y[i] for i in FAR]

    def peer(step):
        return along_z[step // 16] + along_x[step // 4 % 4] + along_y[step % 4]

    peers = range(PEERS - 1, 0, -1)
    odd = lax.rem(section, 2)
    even = odd == 0
    last = section == SECTIONS - 1
    spread = jnp.logical_and(even, section < SECTIONS - 2)
    my_micro, bit = y // 2, lax.rem(y, 2)
    my_block = (1 - bit) * (1 - z) + bit * (2 + z)

    def owner(micro, block):
        return index(lax.rem((block + 1) // 2 + 1, 2), x, 2 * micro + block // 2)

    def remote(src, dst, out, sem, at_section, tp):
        return pltpu.make_async_remote_copy(
            src_ref=src, dst_ref=dst, send_sem=out, recv_sem=sem,
            device_id={"section": at_section, "tp": tp}, device_id_type=MESH,
        )

    def settle(ref, sem):
        pltpu.make_async_copy(ref, ref, sem).wait()

    def columns(tp):
        return pl.ds(pl.multiple_of(tp * WIDTH, WIDTH), WIDTH)

    load_online = pltpu.make_async_copy(online_ref, online, load_sem.at[0])
    load_online.start()

    @pl.when(jnp.logical_not(last))
    def _():
        pltpu.make_async_copy(target_ref, target, load_sem.at[1]).start()

    @pl.when(last)
    def _():
        pltpu.make_async_copy(target_ref.at[me], target.at[me], load_sem.at[1]).start()
        pltpu.make_async_copy(head_ref, moved.at[me], load_sem.at[2]).start()

    @pl.when(section == 0)
    def _():
        for c in range(CHUNKS):
            pltpu.make_async_copy(
                start_ref.at[pl.ds(c * PART, PART)], hidden.at[c, me], own_sem.at[c]
            ).start()

    barrier = pltpu.get_barrier_semaphore()

    def greet(at_section, tp):
        pl.semaphore_signal(
            barrier, inc=1, device_id={"section": at_section, "tp": tp}, device_id_type=MESH
        )

    for step in peers:
        greet(section, peer(step))

    @pl.when(jnp.logical_and(odd == 1, jnp.logical_not(last)))
    def _():
        for step in peers:
            greet(section - 1, peer(step))

    @pl.when(section > 0)
    def _():
        greet(section - 1, me)

    for micro in range(2):
        mine = owner(micro, section // 2)

        @pl.when(jnp.logical_not(jnp.logical_and(last, mine == me)))
        def _():
            greet(SECTIONS - 1, mine)

    @pl.when(spread)
    def _():
        pl.semaphore_wait(barrier, 2 * PEERS - 1)

    @pl.when(jnp.logical_not(jnp.logical_or(spread, last)))
    def _():
        pl.semaphore_wait(barrier, PEERS)

    @pl.when(jnp.logical_and(last, my_block != 3))
    def _():
        pl.semaphore_wait(barrier, PEERS - 1 + 16)

    @pl.when(jnp.logical_and(last, my_block == 3))
    def _():
        pl.semaphore_wait(barrier, PEERS - 1 + 15)

    most = PEERS - 1

    @pl.when(last)
    def _():
        seen = set()

        def near(dx, dy, dz):
            return along_z[dz] + ring_x[dx % 4] + ring_y[dy % 4]

        def arrived(dx, dy, dz):
            if (dx, dy, dz) not in seen:
                seen.add((dx, dy, dz))
                tp = near(dx, dy, dz)
                settle(moved.at[tp], head_sem.at[tp])

        rows = [
            (dx, dy, dz) for dx in (1, 0, 3, 2) for dy in (2, 1, 0, 3) for dz in (1, 0) if (dx, dy, dz) != (0, 0, 0)
        ]

        def give_target(count):
            for _ in range(min(count, len(rows))):
                tp = near(*rows.pop(0))
                remote(target_ref.at[tp], target.at[me], move_out, row_sem.at[me], section, tp).start()

        def pass_on(source, step):
            arrived(*source)
            tp = near(*source)
            remote(moved.at[tp], moved.at[tp], move_out, head_sem.at[tp], section, near(*step)).start()
            give_target(2)

        for dy, dx in ((3, 1), (3, 0), (3, 3), (0, 3), (1, 3), (0, 1), (1, 0), (1, 1), (0, 0)):
            for dz in (0, 1):
                if (dx, dy, dz) != (0, 0, 0):
                    remote(
                        head_ref, moved.at[me], move_out, head_sem.at[me], section, near(dx, dy, dz)
                    ).start()
        give_target(FIRST)
        for dz in (0, 1):
            for dx in (1, 0, 3):
                pass_on((dx, 1, dz), (0, -1, 0))
        for dy in (0, 1, 3, 2):
            for dz in (0, 1):
                pass_on((1, dy, dz), (-1, 0, 0))
        give_target(PEERS)
        load_online.wait()
        settle(target.at[0], load_sem.at[1])
        settle(moved.at[0], load_sem.at[2])
        product_head[...] = jnp.zeros_like(product_head)
        for dx in (0, 1, 3, 2):
            for dz in range(2):
                for dy in range(4):
                    if (dx, dy, dz) != (0, 0, 0):
                        arrived(dx, dy, dz)
                        tp = near(dx, dy, dz)
                        settle(target.at[tp], row_sem.at[tp])

            @pl.loop(0, 8, unroll=2)
            def _(i):
                tp = (i // 4) * 16 + ring_x[dx] + lax.rem(i, 4)
                blended = (
                    0.25 * online[:, columns(tp)].astype(jnp.float32) + 0.75 * target[tp].astype(jnp.float32)
                ).astype(jnp.bfloat16)
                product_head[...] += jnp.dot(blended, moved[tp], preferred_element_type=jnp.float32)

        both[:, :WIDTH] = moved[me]
        both[:, WIDTH:] = product_head[...].astype(jnp.bfloat16)

    lots = [[PEERS - 1 - 8 * group - u for u in range(8)] for group in range(4)]

    def send(c):
        settle(hidden.at[c, 0], own_sem.at[c])

        def partial(own, group):
            return [
                jnp.dot(own, online[:, columns(peer(step))], preferred_element_type=jnp.float32).astype(jnp.bfloat16)
                for step in lots[group]
            ]

        def keep(parts, group):
            for step, part in zip(lots[group], parts):
                if step == 0:
                    shares[c, me] = part
                else:
                    sends[c, peer(step)] = part

        def give(group):
            for step in lots[group]:
                if step > 0:
                    tp = peer(step)
                    remote(
                        sends.at[c, tp], shares.at[c, me], share_out.at[c], share_sem.at[c], section, tp
                    ).start()

        def give_all():
            own = hidden[c, me]
            parts = partial(own, 0)
            for group in range(4):
                keep(parts, group)
                if group < 3:
                    parts = partial(own, group + 1)
                give(group)

        @pl.when(even)
        def _():
            for step in peers:
                remote(
                    hidden.at[c, me], hidden.at[c, me], all_out.at[c], all_sem.at[step // 16, c], section, peer(step)
                ).start()

        give_all()

    def reduce(c):
        @pl.when(c == 0)
        def _():
            settle(target, load_sem.at[1])

        product = jnp.zeros((PART, WIDTH), jnp.float32)
        square = jnp.zeros((PART, WIDTH), jnp.float32)
        for plane in range(2):
            settle(hidden.at[c, pl.ds(0, 15 + plane)], all_sem.at[plane, c])
            for i in range(16):
                tp = along_z[plane] + i
                block = hidden[c, tp]
                product += jnp.dot(block, target[tp], preferred_element_type=jnp.float32)
                wide = block.astype(jnp.float32)
                square += wide * wide
        scale = lax.rsqrt(jnp.sum(square, axis=1, keepdims=True) * (1.0 / DEPTH) + 1e-06)
        own = hidden[c, me].astype(jnp.float32)

        settle(shares.at[c, pl.ds(0, most)], share_sem.at[c])
        total = jnp.zeros((PART, WIDTH), jnp.float32)
        for tp in range(PEERS):
            total += shares[c, tp].astype(jnp.float32)
        result[c] = (own + scale * (0.75 * product + 0.25 * total)).astype(jnp.bfloat16)
        remote(result.at[c], hidden.at[c, me], next_out.at[c], own_sem.at[c], section + 1, me).start()

        @pl.when(spread)
        def _():
            for step in peers:
                remote(
                    result.at[c], hidden.at[c, me], next_out.at[c], all_sem.at[step // 16, c], section + 1, peer(step)
                ).start()

    @pl.when(jnp.logical_not(last))
    def _():
        load_online.wait()
        ahead = jnp.where(section == 0, AHEAD[0], jnp.where(even, AHEAD[2], AHEAD[1]))

        @pl.loop(0, CHUNKS + max(AHEAD))
        def _(step):
            @pl.when(step < CHUNKS)
            def _():
                send(step)

            @pl.when(jnp.logical_and(step >= ahead, step < CHUNKS + ahead))
            def _():
                reduce(step - ahead)

    @pl.when(last)
    def _():
        @pl.loop(0, CHUNKS)
        def _(c):
            settle(hidden.at[c, 0], own_sem.at[c])
            own = hidden[c, me]
            wide = own.astype(jnp.float32)
            scores[c, :, : 2 * WIDTH] = jnp.dot(own, both[...], preferred_element_type=jnp.float32)
            scores[c, :, 2 * WIDTH :] = jnp.broadcast_to(
                jnp.sum(wide * wide, axis=1, keepdims=True), (OWNED, 128)
            )
            first = owner(c // 4, lax.rem(c, 4))
            for column in range(4):
                tp = first + (column - x) * 4

                @pl.when(tp == me)
                def _():
                    gathered[me] = scores[c]

                @pl.when(tp != me)
                def _():
                    remote(scores.at[c], gathered.at[me], score_out, score_sem, section, tp).start()

        settle(gathered.at[pl.ds(0, most)], score_sem)
        total = jnp.zeros((OWNED, SCORE), jnp.float32)
        for tp in range(PEERS):
            total += gathered[tp]
        scale = lax.rsqrt(total[:, 2 * WIDTH : 2 * WIDTH + 1] * (1.0 / DEPTH) + 1e-06)
        summed[...] = total[:, :WIDTH] + scale * total[:, WIDTH : 2 * WIDTH]
        for i in range(16):
            at_section = 2 * my_block + i // 8
            tp = index((i // 4) % 2, x, i % 4)
            local = jnp.logical_and(at_section == section, tp == me)

            @pl.when(local)
            def _():
                pltpu.make_async_copy(summed, finals.at[my_micro], final_sem.at[my_micro]).start()

            @pl.when(jnp.logical_not(local))
            def _():
                remote(
                    summed, finals.at[my_micro], final_out, final_sem.at[my_micro], at_section, tp
                ).start()

    @pl.loop(0, CHUNKS)
    def _(c):
        @pl.when(jnp.logical_not(last))
        def _():
            settle(sends.at[c, pl.ds(0, most)], share_out.at[c])

        @pl.when(even)
        def _():
            settle(hidden.at[c, pl.ds(0, most)], all_out.at[c])

        @pl.when(spread)
        def _():
            settle(hidden.at[c], next_out.at[c])

        @pl.when(jnp.logical_not(jnp.logical_or(spread, last)))
        def _():
            settle(hidden.at[c, 0], next_out.at[c])

    @pl.when(last)
    def _():
        settle(moved.at[pl.ds(0, most)], move_out)
        settle(target.at[pl.ds(0, most)], move_out)

    lane = lax.broadcasted_iota(jnp.int32, (OWNED, WIDTH), 1)
    row = lax.broadcasted_iota(jnp.int32, (OWNED, WIDTH), 0) - 4 * odd
    for micro in range(2):
        settle(finals.at[micro], final_sem.at[micro])
        q = finals[micro]
        action = jnp.zeros((OWNED, WIDTH), jnp.int32)
        for token in range(4):
            action = jnp.where(row == token, action_ref[micro, token], action)
        best = jnp.max(q, axis=1, keepdims=True)
        taken = jnp.sum(jnp.where(lane == action, q, 0.0), axis=1, keepdims=True)
        best = jnp.sum(jnp.where(lane == row, best, 0.0), axis=0, keepdims=True)
        taken = jnp.sum(jnp.where(lane == row, taken, 0.0), axis=0, keepdims=True)
        out_ref[pl.ds(micro, 1), :] = best[:, :4]
        out_ref[pl.ds(2 + micro, 1), :] = taken[:, :4]

    @pl.when(last)
    def _():
        settle(gathered.at[pl.ds(0, most)], score_out)

        @pl.when(my_block != 3)
        def _():
            settle(wide_finals.at[pl.ds(0, 16)], final_out)

        @pl.when(my_block == 3)
        def _():
            settle(wide_finals.at[pl.ds(0, 15)], final_out)


def per_device(start_tokens, target_weight, online_weight, head_weight, reward, action_bin):
    bf16, f32 = jnp.bfloat16, jnp.float32
    dma = pltpu.SemaphoreType.DMA
    micro, share = reward.shape
    anywhere = pl.BlockSpec(memory_space=pl.ANY)
    vmem = pl.BlockSpec(memory_space=pltpu.VMEM)
    blocks = pltpu.VMEM((CHUNKS, PEERS, PART, WIDTH), bf16)
    weight = pltpu.VMEM((PEERS, WIDTH, WIDTH), bf16)
    found = pl.pallas_call(
        kernel,
        out_shape=jax.ShapeDtypeStruct((2 * micro, share), f32),
        in_specs=[anywhere, anywhere, anywhere, anywhere, pl.BlockSpec(memory_space=pltpu.SMEM)],
        out_specs=vmem,
        scratch_shapes=[
            weight,
            pltpu.VMEM((WIDTH, DEPTH), bf16),
            weight,
            blocks,
            blocks,
            blocks,
            pltpu.VMEM((CHUNKS, PART, WIDTH), bf16),
            pltpu.VMEM((WIDTH, WIDTH), f32),
            pltpu.VMEM((WIDTH, 2 * WIDTH), bf16),
            pltpu.VMEM((CHUNKS, OWNED, SCORE), f32),
            pltpu.VMEM((PEERS, OWNED, SCORE), f32),
            pltpu.VMEM((OWNED, WIDTH), f32),
            pltpu.VMEM((2, OWNED, WIDTH), f32),
            pltpu.VMEM((16, OWNED, WIDTH), f32),
            dma((3,)),
            dma((PEERS,)),
            dma((PEERS,)),
            dma((CHUNKS,)),
            dma((2, CHUNKS)),
            dma((CHUNKS,)),
            dma,
            dma((CHUNKS,)),
            dma((CHUNKS,)),
            dma((CHUNKS,)),
            dma,
            dma,
            dma((2,)),
            dma,
        ],
        name="relay",
        compiler_params=pltpu.CompilerParams(
            collective_id=0, has_side_effects=True
        ),
    )(
        start_tokens.reshape(ROWS, WIDTH),
        target_weight.reshape(PEERS, WIDTH, WIDTH),
        online_weight.reshape(WIDTH, DEPTH),
        head_weight,
        action_bin,
    )
    return reward + 0.98 * found[:micro], found[micro:]


def solution(mesh):
    in_specs = (
        P(None, None, "tp"),
        P("section", None, "tp"),
        P("section", "tp", None),
        P("tp", None),
        P(None, "section"),
        P(None, "section"),
    )
    out_specs = (P(None, "section"), P(None, "section"))
    return jax.shard_map(
        per_device, mesh=mesh, in_specs=in_specs, out_specs=out_specs, check_vma=False
    )
```

```python
import jax
import jax.numpy as jnp
from jax import lax
from jax.experimental import pallas as pl
from jax.experimental.pallas import tpu as pltpu
from jax.sharding import PartitionSpec as P

MESH = pl.DeviceIdType.MESH
SECTIONS = 8
PEERS = 32
ROWS = 64
WIDTH = 256
DEPTH = PEERS * WIDTH
CHUNKS = 8
AHEAD = (2, 1, 1)
PART = ROWS // CHUNKS
OWNED = 8
SOURCES = ((0, 3), (1, 2))
SCORE = 2 * WIDTH + 128
FIRST = 4


FAR = (0, 1, 3, 2)


def place(tp):
    return tp // 16, lax.rem(tp // 4, 4), lax.rem(tp, 4)


def index(z, x, y):
    return z * 16 + x * 4 + y


def kernel(
    start_ref, target_ref, online_ref, head_ref, action_ref, out_ref,
    target, online, moved, hidden, shares, sends, result, product_head, both, scores, gathered, summed, finals, wide_finals,
    load_sem, head_sem, row_sem, own_sem, all_sem, share_sem, move_out, all_out, next_out, share_out, score_sem, score_out, final_sem, final_out,
):
    section = lax.axis_index("section")
    me = lax.axis_index("tp")
    z, x, y = place(me)
    along_z = [z * 16, (1 - z) * 16]
    ring_x = [lax.rem(x + i, 4) * 4 for i in range(4)]
    ring_y = [lax.rem(y + i, 4) for i in range(4)]
    along_x = [ring_x[i] for i in FAR]
    along_y = [ring_y[i] for i in FAR]

    def peer(step):
        return along_z[step // 16] + along_x[step // 4 % 4] + along_y[step % 4]

    peers = range(PEERS - 1, 0, -1)
    odd = lax.rem(section, 2)
    even = odd == 0
    last = section == SECTIONS - 1
    spread = jnp.logical_and(even, section < SECTIONS - 2)
    my_micro, bit = y // 2, lax.rem(y, 2)
    my_block = (1 - bit) * (1 - z) + bit * (2 + z)

    def owner(micro, block):
        return index(lax.rem((block + 1) // 2 + 1, 2), x, 2 * micro + block // 2)

    def remote(src, dst, out, sem, at_section, tp):
        return pltpu.make_async_remote_copy(
            src_ref=src, dst_ref=dst, send_sem=out, recv_sem=sem,
            device_id={"section": at_section, "tp": tp}, device_id_type=MESH,
        )

    def settle(ref, sem):
        pltpu.make_async_copy(ref, ref, sem).wait()

    def columns(tp):
        return pl.ds(pl.multiple_of(tp * WIDTH, WIDTH), WIDTH)

    load_online = pltpu.make_async_copy(online_ref, online, load_sem.at[0])
    load_online.start()

    @pl.when(jnp.logical_not(last))
    def _():
        pltpu.make_async_copy(target_ref, target, load_sem.at[1]).start()

    @pl.when(last)
    def _():
        pltpu.make_async_copy(target_ref.at[me], target.at[me], load_sem.at[1]).start()
        pltpu.make_async_copy(head_ref, moved.at[me], load_sem.at[2]).start()

    @pl.when(section == 0)
    def _():
        for c in range(CHUNKS):
            pltpu.make_async_copy(
                start_ref.at[pl.ds(c * PART, PART)], hidden.at[c, me], own_sem.at[c]
            ).start()

    barrier = pltpu.get_barrier_semaphore()

    def greet(at_section, tp):
        pl.semaphore_signal(
            barrier, inc=1, device_id={"section": at_section, "tp": tp}, device_id_type=MESH
        )

    for step in peers:
        greet(section, peer(step))

    @pl.when(jnp.logical_and(odd == 1, jnp.logical_not(last)))
    def _():
        for step in peers:
            greet(section - 1, peer(step))

    @pl.when(section > 0)
    def _():
        greet(section - 1, me)

    for micro in range(2):
        mine = owner(micro, section // 2)

        @pl.when(jnp.logical_not(jnp.logical_and(last, mine == me)))
        def _():
            greet(SECTIONS - 1, mine)

    @pl.when(spread)
    def _():
        pl.semaphore_wait(barrier, 2 * PEERS - 1)

    @pl.when(jnp.logical_not(jnp.logical_or(spread, last)))
    def _():
        pl.semaphore_wait(barrier, PEERS)

    @pl.when(jnp.logical_and(last, my_block != 3))
    def _():
        pl.semaphore_wait(barrier, PEERS - 1 + 16)

    @pl.when(jnp.logical_and(last, my_block == 3))
    def _():
        pl.semaphore_wait(barrier, PEERS - 1 + 15)

    most = PEERS - 1

    @pl.when(last)
    def _():
        seen = set()

        def near(dx, dy, dz):
            return along_z[dz] + ring_x[dx % 4] + ring_y[dy % 4]

        def arrived(dx, dy, dz):
            if (dx, dy, dz) not in seen:
                seen.add((dx, dy, dz))
                tp = near(dx, dy, dz)
                settle(moved.at[tp], head_sem.at[tp])

        rows = [
            (dx, dy, dz) for dx in (1, 0, 3, 2) for dy in (2, 1, 0, 3) for dz in (1, 0) if (dx, dy, dz) != (0, 0, 0)
        ]

        def give_target(count):
            for _ in range(min(count, len(rows))):
                tp = near(*rows.pop(0))
                remote(target_ref.at[tp], target.at[me], move_out, row_sem.at[me], section, tp).start()

        def pass_on(source, step):
            arrived(*source)
            tp = near(*source)
            remote(moved.at[tp], moved.at[tp], move_out, head_sem.at[tp], section, near(*step)).start()
            give_target(2)

        for dy, dx in ((3, 1), (3, 0), (3, 3), (0, 3), (1, 3), (0, 1), (1, 0), (1, 1), (0, 0)):
            for dz in (0, 1):
                if (dx, dy, dz) != (0, 0, 0):
                    remote(
                        head_ref, moved.at[me], move_out, head_sem.at[me], section, near(dx, dy, dz)
                    ).start()
        give_target(FIRST)
        for dz in (0, 1):
            for dx in (1, 0, 3):
                pass_on((dx, 1, dz), (0, -1, 0))
        for dy in (0, 1, 3, 2):
            for dz in (0, 1):
                pass_on((1, dy, dz), (-1, 0, 0))
        give_target(PEERS)
        load_online.wait()
        settle(target.at[0], load_sem.at[1])
        settle(moved.at[0], load_sem.at[2])
        product_head[...] = jnp.zeros_like(product_head)
        for dx in (0, 1, 3, 2):
            for dz in range(2):
                for dy in range(4):
                    if (dx, dy, dz) != (0, 0, 0):
                        arrived(dx, dy, dz)
                        tp = near(dx, dy, dz)
                        settle(target.at[tp], row_sem.at[tp])

            @pl.loop(0, 8, unroll=2)
            def _(i):
                tp = (i // 4) * 16 + ring_x[dx] + lax.rem(i, 4)
                blended = (
                    0.25 * online[:, columns(tp)].astype(jnp.float32) + 0.75 * target[tp].astype(jnp.float32)
                ).astype(jnp.bfloat16)
                product_head[...] += jnp.dot(blended, moved[tp], preferred_element_type=jnp.float32)

        both[:, :WIDTH] = moved[me]
        both[:, WIDTH:] = product_head[...].astype(jnp.bfloat16)

    lots = [[PEERS - 1 - 8 * group - u for u in range(8)] for group in range(4)]

    def send(c):
        settle(hidden.at[c, 0], own_sem.at[c])

        def partial(own, group):
            return [
                jnp.dot(own, online[:, columns(peer(step))], preferred_element_type=jnp.float32).astype(jnp.bfloat16)
                for step in lots[group]
            ]

        def keep(parts, group):
            for step, part in zip(lots[group], parts):
                if step == 0:
                    shares[c, me] = part
                else:
                    sends[c, peer(step)] = part

        def give(group):
            for step in lots[group]:
                if step > 0:
                    tp = peer(step)
                    remote(
                        sends.at[c, tp], shares.at[c, me], share_out.at[c], share_sem.at[c], section, tp
                    ).start()

        def give_all():
            own = hidden[c, me]
            parts = partial(own, 0)
            for group in range(4):
                keep(parts, group)
                if group < 3:
                    parts = partial(own, group + 1)
                give(group)

        @pl.when(even)
        def _():
            for step in peers:
                remote(
                    hidden.at[c, me], hidden.at[c, me], all_out.at[c], all_sem.at[step // 8, c], section, peer(step)
                ).start()

        give_all()

    def reduce(c):
        @pl.when(c == 0)
        def _():
            settle(target, load_sem.at[1])

        product = jnp.zeros((PART, WIDTH), jnp.float32)
        square = jnp.zeros((PART, WIDTH), jnp.float32)
        for quarter in range(4):
            settle(hidden.at[c, pl.ds(0, 7 if quarter == 0 else 8)], all_sem.at[quarter, c])
            for i in range(8):
                tp = along_z[quarter // 2] + ring_x[SOURCES[quarter % 2][i // 4]] + i % 4
                block = hidden[c, tp]
                product += jnp.dot(block, target[tp], preferred_element_type=jnp.float32)
                wide = block.astype(jnp.float32)
                square += wide * wide
        scale = lax.rsqrt(jnp.sum(square, axis=1, keepdims=True) * (1.0 / DEPTH) + 1e-06)
        own = hidden[c, me].astype(jnp.float32)

        settle(shares.at[c, pl.ds(0, most)], share_sem.at[c])
        total = jnp.zeros((PART, WIDTH), jnp.float32)
        for tp in range(PEERS):
            total += shares[c, tp].astype(jnp.float32)
        result[c] = (own + scale * (0.75 * product + 0.25 * total)).astype(jnp.bfloat16)
        remote(result.at[c], hidden.at[c, me], next_out.at[c], own_sem.at[c], section + 1, me).start()

        @pl.when(spread)
        def _():
            for step in peers:
                remote(
                    result.at[c], hidden.at[c, me], next_out.at[c], all_sem.at[step // 8, c], section + 1, peer(step)
                ).start()

    @pl.when(jnp.logical_not(last))
    def _():
        load_online.wait()
        ahead = jnp.where(section == 0, AHEAD[0], jnp.where(even, AHEAD[2], AHEAD[1]))

        @pl.loop(0, CHUNKS + max(AHEAD))
        def _(step):
            @pl.when(step < CHUNKS)
            def _():
                send(step)

            @pl.when(jnp.logical_and(step >= ahead, step < CHUNKS + ahead))
            def _():
                reduce(step - ahead)

    @pl.when(last)
    def _():
        @pl.loop(0, CHUNKS)
        def _(c):
            settle(hidden.at[c, 0], own_sem.at[c])
            own = hidden[c, me]
            wide = own.astype(jnp.float32)
            scores[c, :, : 2 * WIDTH] = jnp.dot(own, both[...], preferred_element_type=jnp.float32)
            scores[c, :, 2 * WIDTH :] = jnp.broadcast_to(
                jnp.sum(wide * wide, axis=1, keepdims=True), (OWNED, 128)
            )
            first = owner(c // 4, lax.rem(c, 4))
            for column in range(4):
                tp = first + (column - x) * 4

                @pl.when(tp == me)
                def _():
                    gathered[me] = scores[c]

                @pl.when(tp != me)
                def _():
                    remote(scores.at[c], gathered.at[me], score_out, score_sem, section, tp).start()

        settle(gathered.at[pl.ds(0, most)], score_sem)
        total = jnp.zeros((OWNED, SCORE), jnp.float32)
        for tp in range(PEERS):
            total += gathered[tp]
        scale = lax.rsqrt(total[:, 2 * WIDTH : 2 * WIDTH + 1] * (1.0 / DEPTH) + 1e-06)
        summed[...] = total[:, :WIDTH] + scale * total[:, WIDTH : 2 * WIDTH]
        for i in range(16):
            at_section = 2 * my_block + i // 8
            tp = index((i // 4) % 2, x, i % 4)
            local = jnp.logical_and(at_section == section, tp == me)

            @pl.when(local)
            def _():
                pltpu.make_async_copy(summed, finals.at[my_micro], final_sem.at[my_micro]).start()

            @pl.when(jnp.logical_not(local))
            def _():
                remote(
                    summed, finals.at[my_micro], final_out, final_sem.at[my_micro], at_section, tp
                ).start()

    @pl.loop(0, CHUNKS)
    def _(c):
        @pl.when(jnp.logical_not(last))
        def _():
            settle(sends.at[c, pl.ds(0, most)], share_out.at[c])

        @pl.when(even)
        def _():
            settle(hidden.at[c, pl.ds(0, most)], all_out.at[c])

        @pl.when(spread)
        def _():
            settle(hidden.at[c], next_out.at[c])

        @pl.when(jnp.logical_not(jnp.logical_or(spread, last)))
        def _():
            settle(hidden.at[c, 0], next_out.at[c])

    @pl.when(last)
    def _():
        settle(moved.at[pl.ds(0, most)], move_out)
        settle(target.at[pl.ds(0, most)], move_out)

    lane = lax.broadcasted_iota(jnp.int32, (OWNED, WIDTH), 1)
    row = lax.broadcasted_iota(jnp.int32, (OWNED, WIDTH), 0) - 4 * odd
    for micro in range(2):
        settle(finals.at[micro], final_sem.at[micro])
        q = finals[micro]
        action = jnp.zeros((OWNED, WIDTH), jnp.int32)
        for token in range(4):
            action = jnp.where(row == token, action_ref[micro, token], action)
        best = jnp.max(q, axis=1, keepdims=True)
        taken = jnp.sum(jnp.where(lane == action, q, 0.0), axis=1, keepdims=True)
        best = jnp.sum(jnp.where(lane == row, best, 0.0), axis=0, keepdims=True)
        taken = jnp.sum(jnp.where(lane == row, taken, 0.0), axis=0, keepdims=True)
        out_ref[pl.ds(micro, 1), :] = best[:, :4]
        out_ref[pl.ds(2 + micro, 1), :] = taken[:, :4]

    @pl.when(last)
    def _():
        settle(gathered.at[pl.ds(0, most)], score_out)

        @pl.when(my_block != 3)
        def _():
            settle(wide_finals.at[pl.ds(0, 16)], final_out)

        @pl.when(my_block == 3)
        def _():
            settle(wide_finals.at[pl.ds(0, 15)], final_out)


def per_device(start_tokens, target_weight, online_weight, head_weight, reward, action_bin):
    bf16, f32 = jnp.bfloat16, jnp.float32
    dma = pltpu.SemaphoreType.DMA
    micro, share = reward.shape
    anywhere = pl.BlockSpec(memory_space=pl.ANY)
    vmem = pl.BlockSpec(memory_space=pltpu.VMEM)
    blocks = pltpu.VMEM((CHUNKS, PEERS, PART, WIDTH), bf16)
    weight = pltpu.VMEM((PEERS, WIDTH, WIDTH), bf16)
    found = pl.pallas_call(
        kernel,
        out_shape=jax.ShapeDtypeStruct((2 * micro, share), f32),
        in_specs=[anywhere, anywhere, anywhere, anywhere, pl.BlockSpec(memory_space=pltpu.SMEM)],
        out_specs=vmem,
        scratch_shapes=[
            weight,
            pltpu.VMEM((WIDTH, DEPTH), bf16),
            weight,
            blocks,
            blocks,
            blocks,
            pltpu.VMEM((CHUNKS, PART, WIDTH), bf16),
            pltpu.VMEM((WIDTH, WIDTH), f32),
            pltpu.VMEM((WIDTH, 2 * WIDTH), bf16),
            pltpu.VMEM((CHUNKS, OWNED, SCORE), f32),
            pltpu.VMEM((PEERS, OWNED, SCORE), f32),
            pltpu.VMEM((OWNED, WIDTH), f32),
            pltpu.VMEM((2, OWNED, WIDTH), f32),
            pltpu.VMEM((16, OWNED, WIDTH), f32),
            dma((3,)),
            dma((PEERS,)),
            dma((PEERS,)),
            dma((CHUNKS,)),
            dma((4, CHUNKS)),
            dma((CHUNKS,)),
            dma,
            dma((CHUNKS,)),
            dma((CHUNKS,)),
            dma((CHUNKS,)),
            dma,
            dma,
            dma((2,)),
            dma,
        ],
        name="relay",
        compiler_params=pltpu.CompilerParams(
            collective_id=0, has_side_effects=True
        ),
    )(
        start_tokens.reshape(ROWS, WIDTH),
        target_weight.reshape(PEERS, WIDTH, WIDTH),
        online_weight.reshape(WIDTH, DEPTH),
        head_weight,
        action_bin,
    )
    return reward + 0.98 * found[:micro], found[micro:]


def solution(mesh):
    in_specs = (
        P(None, None, "tp"),
        P("section", None, "tp"),
        P("section", "tp", None),
        P("tp", None),
        P(None, "section"),
        P(None, "section"),
    )
    out_specs = (P(None, "section"), P(None, "section"))
    return jax.shard_map(
        per_device, mesh=mesh, in_specs=in_specs, out_specs=out_specs, check_vma=False
    )
```
